32 devices in a mesh: leaf: 4 (over y, x), row: 2 (over core), col: 4 (over z).
Axes of the slice: x: 2, y: 2, z: 4, core: 2. Of those that a mesh axis runs over, the one named last changes fastest.
Arguments:
- child_source: float32 [4, 4096, 384], P('leaf', 'col'), may hold values from -6 to 6
- middle_source: float32 [4, 4096, 384], P('leaf', 'col'), may hold values from -6 to 6
- root_source: float32 [16384, 384], P(('leaf', 'col')), may hold values from -6 to 6
- child_inverse: float32 [4, 4096, 4096], P('leaf', 'row', 'col'), may hold values from -0.09375 to 0.09375
- child_update: float32 [4, 2048, 4096], P('leaf', 'col', 'row'), may hold values from -0.09375 to 0.09375
- middle_inverse: float32 [4, 8192, 4096], P('leaf', 'row', 'col'), may hold values from -0.0625 to 0.0625
- middle_update: float32 [4, 2048, 8192], P('leaf', 'col', 'row'), may hold values from -0.0625 to 0.0625
- root_inverse: float32 [16384, 16384], P('row', ('leaf', 'col')), may hold values from -0.046875 to 0.046875
- child_diagmask: int32 [4, 32, 32], P('leaf', 'row', 'col'), may hold values 0 or 1
- child_updmask: int32 [4, 16, 32], P('leaf', 'col', 'row'), may hold values 0 or 1
- middle_diagmask: int32 [4, 64, 32], P('leaf', 'row', 'col'), may hold values 0 or 1
- middle_updmask: int32 [4, 16, 64], P('leaf', 'col', 'row'), may hold values 0 or 1
- root_diagmask: int32 [128, 128], P('row', ('leaf', 'col')), may hold values 0 or 1
- child_rowmap: int32 [4, 2048], replicated, may hold values from 0 to 8191
- middle_rowmap: int32 [2, 4096], replicated, may hold values from 0 to 16383
Outputs:
- child_solution: float32 [4, 4096, 384], P('leaf', 'row', 'col')
- middle_solution: float32 [4, 8192, 192], P('leaf', 'row', 'col')
- root_solution: float32 [16384, 384], P('row', 'col')
The draws below stay inside these ranges and needn't reach their ends.
All inputs are finite; a program needn't handle non-finite values. No bound on the sum of `child_diagmask` or of `child_updmask` or of `middle_diagmask` or of `middle_updmask` or of `root_diagmask` on one device may be relied on, other than what follows from the above.
Results may differ from the reference program's by a relative error of at most 0.0001.
Values sent between devices are 32-bit elements; how exact they have to be, the bound alone decides.
No kernel may reach another device: no remote copies, remote signals or barrier semaphores. Data moves between devices by JAX's collectives and lax.ppermute only.
A program may use at most 192 MiB of HBM per device.

```python
import jax
import jax.numpy as jnp
from jax import lax

BLK = 128
P0 = 4096
U0 = 2048
P1 = 8192
U1 = 4096
P2 = 16384
NRHS = 384


def with_ends(entries, own_key, low, high):
    spot = [jax.random.randint(jax.random.fold_in(own_key, axis), (), 0, length) for axis, length in enumerate(entries.shape)]
    main_axis = entries.shape.index(max(entries.shape))
    next_to = spot[:main_axis] + [(spot[main_axis] + 1) % entries.shape[main_axis]] + spot[main_axis + 1:]
    return entries.at[tuple(spot)].set(low).at[tuple(next_to)].set(high)


def steps_of(key, dims, pieces, least, largest):
    factor_of = 1.0
    for dim, parts in pieces:
        draws = jax.random.uniform(jax.random.fold_in(jax.random.fold_in(key, 6), dim), (parts,), jnp.float32, least / len(pieces), largest / len(pieces))
        factor_of = factor_of * jnp.repeat(jnp.exp(draws), dims[dim] // parts).reshape((-1,) + (1,) * (len(dims) - 1 - dim))
    return factor_of


def bell_draw(rng, extent, width, most, cuts=(), held_as=jnp.bfloat16):
    entries = jax.random.normal(rng, extent, jnp.float32) * width
    if len(cuts) > 0:
        entries = steps_of(rng, extent, cuts, -0.22, 0.18) * entries
    return jnp.clip(entries, min=-most, max=most).astype(held_as)


def setup_inputs(seed: int = 0) -> dict:
    arg_keys = jax.random.split(jax.random.key(seed), 16)
    return {
        "child_source": bell_draw(arg_keys[0], (4, P0, NRHS), 1.0, 6.0, ((0, 4), (1, 4)), jnp.float32),
        "middle_source": bell_draw(arg_keys[1], (4, P1 // 2, NRHS), 1.0, 6.0, ((0, 4), (1, 4)), jnp.float32),
        "root_source": bell_draw(arg_keys[2], (P2, NRHS), 1.0, 6.0, ((0, 16),), jnp.float32),
        "child_inverse": bell_draw(arg_keys[3], (4, P0, P0), P0 ** -0.5, 0.09375, ((0, 4), (1, 2), (2, 4)), jnp.float32),
        "child_update": bell_draw(arg_keys[4], (4, U0, P0), P0 ** -0.5, 0.09375, ((0, 4), (1, 4), (2, 2)), jnp.float32),
        "middle_inverse": bell_draw(arg_keys[5], (4, P1, P1 // 2), P1 ** -0.5, 0.0625, ((0, 4), (1, 2), (2, 4)), jnp.float32),
        "middle_update": bell_draw(arg_keys[6], (4, U1 // 2, P1), P1 ** -0.5, 0.0625, ((0, 4), (1, 4), (2, 2)), jnp.float32),
        "root_inverse": bell_draw(arg_keys[7], (P2, P2), P2 ** -0.5, 0.046875, ((0, 2), (1, 16)), jnp.float32),
        "child_diagmask": with_ends((jax.random.randint(arg_keys[8], (4, P0 // BLK, P0 // BLK), 0, 2) < 1).astype(jnp.int32), jax.random.fold_in(arg_keys[8], 1), 0, 1),
        "child_updmask": with_ends((jax.random.randint(arg_keys[9], (4, U0 // BLK, P0 // BLK), 0, 2) < 1).astype(jnp.int32), jax.random.fold_in(arg_keys[9], 1), 0, 1),
        "middle_diagmask": with_ends((jax.random.randint(arg_keys[10], (4, P1 // BLK, P1 // (2 * BLK)), 0, 2) < 1).astype(jnp.int32), jax.random.fold_in(arg_keys[10], 1), 0, 1),
        "middle_updmask": with_ends((jax.random.randint(arg_keys[11], (4, U1 // (2 * BLK), P1 // BLK), 0, 2) < 1).astype(jnp.int32), jax.random.fold_in(arg_keys[11], 1), 0, 1),
        "root_diagmask": with_ends((jax.random.randint(arg_keys[12], (P2 // BLK, P2 // BLK), 0, 2) < 1).astype(jnp.int32), jax.random.fold_in(arg_keys[12], 1), 0, 1),
        "child_rowmap": with_ends(jax.random.randint(arg_keys[13], (4, U0), 0, P1), jax.random.fold_in(arg_keys[13], 1), 0, P1 - 1).astype(jnp.int32),
        "middle_rowmap": with_ends(jax.random.randint(arg_keys[14], (2, U1), 0, P2), jax.random.fold_in(arg_keys[14], 1), 0, P2 - 1).astype(jnp.int32),
    }


def expand(blocks):
    return jnp.repeat(jnp.repeat(blocks, BLK, axis=0), BLK, axis=1)


def keep_lower(pattern):
    rows_count, cols_count = pattern.shape
    row_ids = jnp.arange(rows_count)[:, None]
    col_ids = jnp.arange(cols_count)[None, :]
    keep = (row_ids == col_ids) | ((row_ids > col_ids) & (pattern == 1))
    return expand(keep.astype(jnp.float32))


def masked_product(panel, keep, vector):
    return jnp.dot(panel * keep, vector, precision=lax.Precision.HIGHEST, preferred_element_type=jnp.float32)


def reference(child_source, middle_source, root_source, child_inverse, child_update, middle_inverse, middle_update, root_inverse, child_diagmask, child_updmask, middle_diagmask, middle_updmask, root_diagmask, child_rowmap, middle_rowmap):
    child_values = []
    child_lifts = []
    for child in range(4):
        solved = masked_product(child_inverse[child], keep_lower(child_diagmask[child]), child_source[child])
        child_values.append(solved)
        child_lifts.append(masked_product(child_update[child], expand(child_updmask[child].astype(jnp.float32)), solved))
    middle_values = []
    middle_lifts = []
    for middle in range(2):
        assembled = jnp.concatenate([middle_source[2 * middle], middle_source[2 * middle + 1]], axis=0)
        for half in range(2):
            assembled = assembled.at[child_rowmap[2 * middle + half]].add(child_lifts[2 * middle + half])
        inverse = jnp.concatenate([middle_inverse[2 * middle], middle_inverse[2 * middle + 1]], axis=1)
        pattern = jnp.concatenate([middle_diagmask[2 * middle], middle_diagmask[2 * middle + 1]], axis=1)
        solved = masked_product(inverse, keep_lower(pattern), assembled)
        middle_values.append(solved[:, : NRHS // 2])
        middle_values.append(solved[:, NRHS // 2:])
        update = jnp.concatenate([middle_update[2 * middle], middle_update[2 * middle + 1]], axis=0)
        upattern = jnp.concatenate([middle_updmask[2 * middle], middle_updmask[2 * middle + 1]], axis=0)
        middle_lifts.append(masked_product(update, expand(upattern.astype(jnp.float32)), solved))
    assembled = root_source
    for middle in range(2):
        assembled = assembled.at[middle_rowmap[middle]].add(middle_lifts[middle])
    root_solution = masked_product(root_inverse, keep_lower(root_diagmask), assembled)
    return jnp.stack(child_values), jnp.stack(middle_values), root_solution
```

```python
import functools

import jax
import jax.numpy as jnp
from jax import lax
from jax.experimental import pallas as pl
from jax.experimental.pallas import tpu as pltpu
from jax.sharding import PartitionSpec as P


BLK = 128
CHILD_CHUNKS = 4
MIDDLE_CHUNKS = 4
ROOT_CHUNKS = 8
VMEM_BYTES = 56 * 2**20


def swapped(value, dim):
    axis, bit = dim
    pairs = [(source, source ^ (1 << bit)) for source in range(lax.axis_size(axis))]
    return lax.ppermute(value, axis, pairs)


def bit_of(dim):
    axis, bit = dim
    return (lax.axis_index(axis) >> bit) & 1


def bits_of(axis):
    return [(axis, bit) for bit in reversed(range(lax.axis_size(axis).bit_length() - 1))]


def block_order(dims, first, weights=None):
    n = len(dims)
    weights = weights or [1 << (n - 1 - j) for j in range(n)]
    mine = sum(bit_of(dim) * weight for dim, weight in zip(dims, weights, strict=True))
    order = []
    for place in range(1 << n):
        apart = sum(w for j, w in enumerate(weights) if not (place >> (n - 1 - j)) & 1)
        order.append(first + (mine ^ apart))
    return order


def exchange_stages(send, keep, dims):
    for j, dim in enumerate(dims):
        came = swapped(send, dim)
        if j == len(dims) - 1:
            value = keep + came
        else:
            h = keep.shape[0] // 2
            send, keep = keep[:h] + came[:h], keep[h:] + came[h:]
    for dim in reversed(dims):
        came = swapped(value, dim)
        value = jnp.concatenate([came, value], 0)
    return value


def reduce_scatter(send, keep, dims):
    for j, dim in enumerate(dims):
        came = swapped(send, dim)
        if j == len(dims) - 1:
            return keep + came
        h = keep.shape[0] // 2
        send, keep = keep[:h] + came[:h], keep[h:] + came[h:]
    return keep


def in_order(value, dims):
    shape = value.shape
    value = value.reshape((2,) * len(dims) + (-1,) + shape[1:])
    for j, dim in enumerate(dims):
        value = jnp.where(bit_of(dim) == 0, jnp.flip(value, j), value)
    return value.reshape(shape)


def split_into(target, value, width):
    high = value.astype(jnp.bfloat16)
    target[:, :width] = high
    target[:, width:] = (value - high.astype(jnp.float32)).astype(jnp.bfloat16)


def panel_kernel(unit, merge, depth, cols_all, order, flags, *refs):
    panels, (x, send, keep, xs, high, low) = refs[:merge], refs[merge:]
    width = x.shape[1]
    i = pl.program_id(0)

    @pl.when(i == 0)
    def _():
        split_into(xs, x[...], width)

    bs = min(unit, BLK)
    for u, panel in enumerate(panels):
        for b in range(unit // bs):
            row_block = (order[i * merge + u] * unit + b * bs) // BLK
            rows = slice(b * bs, (b + 1) * bs)
            into = slice(u * unit + b * bs, u * unit + (b + 1) * bs)
            for kb in range(depth // BLK):
                cols = slice(kb * BLK, (kb + 1) * BLK)
                flag = flags[row_block * cols_all + kb].astype(jnp.float32)
                kept = panel[rows, cols] * flag
                top = kept.astype(jnp.bfloat16)
                high[into, cols] = top
                low[into, cols] = (kept - top.astype(jnp.float32)).astype(jnp.bfloat16)
    both = jnp.dot(high[...], xs[...], preferred_element_type=jnp.float32)
    rest_of = jnp.dot(low[...], xs[:, :width], preferred_element_type=jnp.float32)
    result = both[:, :width] + (both[:, width:] + rest_of)

    @pl.when(i < pl.num_programs(0) // 2)
    def _():
        send[...] = result

    @pl.when(i >= pl.num_programs(0) // 2)
    def _():
        keep[...] = result


def panel_product(panel, flags, x, order, unit):
    depth, width = x.shape
    _, cols = panel.shape
    half = len(order) // 2
    merge = 1
    while merge * 2 <= half and merge * 2 * unit <= 512:
        merge *= 2
    steps = half // merge

    def place(start):
        return lambda i, order, flags: (jnp.clip(i - start, 0, steps - 1), 0)

    def source(u):
        return lambda i, order, flags: (order[i * merge + u], 0)

    in_specs = [pl.BlockSpec((unit, depth), source(u)) for u in range(merge)]
    in_specs.append(pl.BlockSpec((depth, width), lambda i, order, flags: (0, 0)))
    n = len(order)
    return pl.pallas_call(
        functools.partial(panel_kernel, unit, merge, depth, cols // BLK),
        grid_spec=pltpu.PrefetchScalarGridSpec(
            num_scalar_prefetch=2,
            grid=(2 * steps,),
            in_specs=in_specs,
            out_specs=[pl.BlockSpec((merge * unit, width), place(s)) for s in (0, steps)],
            scratch_shapes=[
                pltpu.VMEM((depth, 2 * width), jnp.bfloat16),
                pltpu.VMEM((merge * unit, depth), jnp.bfloat16),
                pltpu.VMEM((merge * unit, depth), jnp.bfloat16),
            ],
        ),
        out_shape=[jax.ShapeDtypeStruct((half * unit, width), jnp.float32)] * 2,
        compiler_params=pltpu.CompilerParams(vmem_limit_bytes=VMEM_BYTES),
        cost_estimate=pl.CostEstimate(
            flops=6 * n * unit * depth * width,
            bytes_accessed=4 * n * unit * (depth + width) + 4 * depth * width,
            transcendentals=0,
        ),
    )(jnp.stack(order).astype(jnp.int32), flags, *([panel] * merge), x)


def update_kernel(unit, k_first, cols_all, with_acc, order, flags, panel, x, *rest):
    acc = rest[0] if with_acc else None
    out, xs, high, low, total = rest[-5:]
    rows, depth = panel.shape
    width = x.shape[1]
    i = pl.program_id(0)
    split_into(xs, x[...], width)
    bs = min(rows, BLK)
    for b in range(rows // bs):
        band = slice(b * bs, (b + 1) * bs)
        for kb in range(depth // BLK):
            cols = slice(kb * BLK, (kb + 1) * BLK)
            place = (b * bs // BLK) * cols_all + k_first + i * (depth // BLK) + kb
            kept = panel[band, cols] * flags[place].astype(jnp.float32)
            top = kept.astype(jnp.bfloat16)
            high[band, cols] = top
            low[band, cols] = (kept - top.astype(jnp.float32)).astype(jnp.bfloat16)
    both = jnp.dot(high[...], xs[...], preferred_element_type=jnp.float32)
    rest_of = jnp.dot(low[...], xs[:, :width], preferred_element_type=jnp.float32)
    result = both[:, :width] + (both[:, width:] + rest_of)

    @pl.when(i == 0)
    def _():
        total[...] = result

    @pl.when(i > 0)
    def _():
        total[...] += result

    @pl.when(i == pl.num_programs(0) - 1)
    def _():
        for j in range(rows // unit):
            there = pl.ds(pl.multiple_of(order[j] * unit, unit), unit)
            value = total[j * unit : (j + 1) * unit, :]
            if with_acc:
                value = value + acc[there, :]
            out[there, :] = value


def update_product(panel, flags, x, order, chunk, acc=None):
    depth, width = x.shape
    rows, cols = panel.shape
    tile = min(depth, 512)
    steps = depth // tile
    whole = pl.BlockSpec((rows, width), lambda i, order, flags: (0, 0))
    in_specs = [
        pl.BlockSpec((rows, tile), lambda i, order, flags: (0, chunk * steps + i)),
        pl.BlockSpec((tile, width), lambda i, order, flags: (i, 0)),
    ]
    args = [panel, x]
    if acc is not None:
        in_specs.append(whole)
        args.append(acc)
    kernel = functools.partial(
        update_kernel, rows // len(order), chunk * (depth // BLK), cols // BLK, acc is not None
    )
    return pl.pallas_call(
        kernel,
        grid_spec=pltpu.PrefetchScalarGridSpec(
            num_scalar_prefetch=2,
            grid=(steps,),
            in_specs=in_specs,
            out_specs=whole,
            scratch_shapes=[
                pltpu.VMEM((tile, 2 * width), jnp.bfloat16),
                pltpu.VMEM((rows, tile), jnp.bfloat16),
                pltpu.VMEM((rows, tile), jnp.bfloat16),
                pltpu.VMEM((rows, width), jnp.float32),
            ],
        ),
        out_shape=jax.ShapeDtypeStruct((rows, width), jnp.float32),
        compiler_params=pltpu.CompilerParams(vmem_limit_bytes=VMEM_BYTES),
        cost_estimate=pl.CostEstimate(
            flops=6 * rows * depth * width,
            bytes_accessed=4 * (rows * depth + rows * width + depth * width),
            transcendentals=0,
        ),
    )(jnp.stack(order).astype(jnp.int32), flags, *args)


def turn_kernel(order, keep_a, came_a, keep_b, came_b, send, keep, whole):
    h = keep_a.shape[0]
    whole[:, :h] = (keep_a[...] + came_a[...]).T
    whole[:, h:] = (keep_b[...] + came_b[...]).T
    count = order.shape[0]
    share = whole.shape[0] // count
    for place in range(count):
        out = send if place < count // 2 else keep
        at = place % (count // 2) * share
        out[at : at + share, :] = whole[pl.ds(pl.multiple_of(order[place] * share, share), share), :]


def turned_sums(order, *parts):
    rows, width = parts[0].shape
    whole = pl.BlockSpec((rows, width), lambda i, order: (0, 0))
    half = pl.BlockSpec((width // 2, 2 * rows), lambda i, order: (0, 0))
    return pl.pallas_call(
        turn_kernel,
        grid_spec=pltpu.PrefetchScalarGridSpec(
            num_scalar_prefetch=1,
            grid=(1,),
            in_specs=[whole] * 4,
            out_specs=[half, half],
            scratch_shapes=[pltpu.VMEM((width, 2 * rows), jnp.float32)],
        ),
        out_shape=[jax.ShapeDtypeStruct((width // 2, 2 * rows), jnp.float32)] * 2,
        compiler_params=pltpu.CompilerParams(vmem_limit_bytes=VMEM_BYTES),
        cost_estimate=pl.CostEstimate(
            flops=2 * rows * width, bytes_accessed=24 * rows * width, transcendentals=0
        ),
    )(jnp.stack(order).astype(jnp.int32), *parts)


def finish_kernel(leaf, *refs):
    pieces, out = refs[:4], refs[-1]
    unit = out.shape[1]
    i = pl.program_id(0)
    for k, piece in enumerate(pieces):
        for h in range(2):

            @pl.when(i == 2 * k + h)
            def _(piece=piece, h=h):
                out[...] = piece[:, h * unit : (h + 1) * unit]


def finished_rows(pieces, pair, leaf_index, rows, before):
    width, both = pieces[0].shape
    unit = both // 2
    whole = pl.BlockSpec((width, both), lambda i, leaf: (0, 0))
    in_specs, args = [whole] * 4, list(pieces)
    aliases = {}
    if before is not None:
        in_specs.append(pl.BlockSpec(memory_space=pl.ANY))
        args.append(before)
        aliases = {5: 0}
    return pl.pallas_call(
        finish_kernel,
        grid_spec=pltpu.PrefetchScalarGridSpec(
            num_scalar_prefetch=1,
            grid=(8,),
            in_specs=in_specs,
            out_specs=pl.BlockSpec(
                (width, unit), lambda i, leaf: (0, (2 * pair + i % 2) * 4 + (leaf[0] ^ (i // 2)))
            ),
        ),
        out_shape=jax.ShapeDtypeStruct((width, rows), jnp.float32),
        input_output_aliases=aliases,
        cost_estimate=pl.CostEstimate(flops=0, bytes_accessed=64 * unit * width, transcendentals=0),
    )(jnp.reshape(leaf_index, (1,)).astype(jnp.int32), *args)


def place_kernel(targets, lifts, out, total, split):
    i = pl.program_id(0)
    width = lifts.shape[1]

    @pl.when(i == 0)
    def _():
        total[...] = jnp.zeros_like(total)

    split_into(split, lifts[...], width)
    shape = (total.shape[0], lifts.shape[0])
    hits = lax.broadcasted_iota(jnp.int32, shape, 0) == targets[0]
    hits = jnp.where(hits, 1.0, 0.0).astype(jnp.bfloat16)
    total[...] += jnp.dot(hits, split[...], preferred_element_type=jnp.float32)

    @pl.when(i == pl.num_programs(0) - 1)
    def _():
        out[...] = total[:, :width] + total[:, width:]


def placed_rows(lifts, targets, count):
    total, width = lifts.shape
    tile = min(total, 512)
    return pl.pallas_call(
        place_kernel,
        grid=(total // tile,),
        in_specs=[
            pl.BlockSpec((1, 1, tile), lambda i: (i, 0, 0)),
            pl.BlockSpec((tile, width), lambda i: (i, 0)),
        ],
        out_specs=pl.BlockSpec((count, width), lambda i: (0, 0)),
        out_shape=jax.ShapeDtypeStruct((count, width), jnp.float32),
        scratch_shapes=[
            pltpu.VMEM((count, 2 * width), jnp.float32),
            pltpu.VMEM((tile, 2 * width), jnp.bfloat16),
        ],
        compiler_params=pltpu.CompilerParams(vmem_limit_bytes=VMEM_BYTES),
        cost_estimate=pl.CostEstimate(
            flops=4 * total * count * width, bytes_accessed=4 * width * (total + count), transcendentals=0
        ),
    )(targets.reshape(total // tile, 1, tile), lifts)


def lower_flags(pattern, row_first, col_first):
    rows, cols = pattern.shape
    row_ids = row_first + jnp.arange(rows, dtype=jnp.int32)[:, None]
    col_ids = col_first + jnp.arange(cols, dtype=jnp.int32)[None, :]
    keep = (row_ids == col_ids) | (row_ids > col_ids) & (pattern == 1)
    return keep.astype(jnp.int32).reshape(-1)


def gather_line(own, dims):
    pieces = {0: own}
    for axis, bit in dims:
        for k in list(pieces):
            pieces[k ^ (1 << bit)] = swapped(pieces[k], (axis, bit))
    return [pieces[k] for k in range(len(pieces))]


def relative(table, axis, dim):
    for bit in range(table.shape[axis].bit_length() - 1):
        shape = table.shape
        cut = shape[:axis] + (shape[axis] >> (bit + 1), 2, 1 << bit) + shape[axis + 1 :]
        parts = table.reshape(cut)
        own = (dim >> bit) & 1
        table = jnp.where(own == 1, jnp.flip(parts, axis + 1), parts).reshape(shape)
    return table


def row_sum(value, row_dims):
    for dim in row_dims:
        value = value + swapped(value, dim)
    return value


def local(
    child_source,
    middle_source,
    root_source,
    child_inverse,
    child_update,
    middle_inverse,
    middle_update,
    root_inverse,
    child_diagmask,
    child_updmask,
    middle_diagmask,
    middle_updmask,
    root_diagmask,
    child_rowmap,
    middle_rowmap,
):
    leaf_index = lax.axis_index("leaf")
    row_index = lax.axis_index("row")
    col_index = lax.axis_index("col")
    n_leaf = lax.axis_size("leaf")
    n_row = lax.axis_size("row")
    n_col = lax.axis_size("col")
    half = leaf_index % 2
    couple = leaf_index // 2
    nrhs = child_source.shape[2]
    half_dim, couple_dim = ("leaf", 0), ("leaf", 1)
    row_dims = bits_of("row")
    col_dims = bits_of("col")
    near_first = list(reversed(col_dims))

    child_rows, child_cols = child_inverse.shape[1:]
    middle_rows, middle_cols = middle_inverse.shape[1:]
    root_rows, root_cols = root_inverse.shape
    middle_first = (half * n_col + col_index) * middle_cols
    root_first = (leaf_index * n_col + col_index) * root_cols

    child_flags = lower_flags(
        child_diagmask[0], row_index * (child_rows // BLK), col_index * (child_cols // BLK)
    )
    middle_flags = lower_flags(
        middle_diagmask[0], row_index * (middle_rows // BLK), middle_first // BLK
    )
    root_flags = lower_flags(root_diagmask, row_index * (root_rows // BLK), root_first // BLK)
    child_upd_flags = child_updmask[0].reshape(-1)
    middle_upd_flags = middle_updmask[0].reshape(-1)

    child_lift_rows = child_update.shape[1]
    middle_lift_rows = middle_update.shape[1]
    pair_targets = lax.dynamic_slice_in_dim(child_rowmap, 2 * couple, 2, 0)
    pair_targets = pair_targets.reshape(2, n_col, n_row, child_lift_rows // n_row)
    pair_targets = lax.dynamic_index_in_dim(pair_targets, row_index, 2, False)
    pair_targets = relative(relative(pair_targets, 0, half), 1, col_index)
    pair_targets = pair_targets.transpose(1, 0, 2).reshape(-1) - middle_first
    root_targets = middle_rowmap.reshape(n_leaf, n_col, n_row, middle_lift_rows // n_row)
    root_targets = lax.dynamic_index_in_dim(root_targets, row_index, 2, False)
    root_targets = relative(relative(root_targets, 0, leaf_index), 1, col_index)
    root_targets = root_targets.transpose(1, 0, 2).reshape(-1) - root_first

    def chunked(panel, flags, x, dims, chunks, update, update_flags):
        rows = panel.shape[0]
        count = 1 << len(dims)
        chunks = max(1, min(chunks, rows // (count * BLK)))
        unit = rows // chunks // count
        lift_order = block_order(row_dims, 0)
        values, lift, partials = [], None, []
        for c in range(chunks):
            order = block_order(dims, c * count)
            partials.append(panel_product(panel, flags, x, order, unit))
        for c in range(chunks):
            value = exchange_stages(*partials[c], dims)
            values.append(in_order(value, dims))
        for c in range(chunks):
            lift = update_product(update, update_flags, values[c], lift_order, c, lift)
        h = lift.shape[0] // 2
        return jnp.concatenate(values, 0), reduce_scatter(lift[:h], lift[h:], row_dims)

    child_value, child_lift = chunked(
        child_inverse[0], child_flags, child_source[0], near_first, CHILD_CHUNKS,
        child_update[0], child_upd_flags,
    )
    pieces = []
    for piece in gather_line(child_lift, col_dims):
        pieces += [piece, swapped(piece, half_dim)]
    added = placed_rows(jnp.concatenate(pieces, 0), pair_targets, middle_cols)
    middle_rhs = middle_source[0] + row_sum(added, row_dims)

    middle_value, middle_lift = chunked(
        middle_inverse[0], middle_flags, middle_rhs, [half_dim] + near_first, MIDDLE_CHUNKS,
        middle_update[0], middle_upd_flags,
    )
    pieces = []
    for piece in gather_line(middle_lift, col_dims):
        h = piece.shape[0] // 2
        by_half = swapped(piece, half_dim)
        by_couple = swapped(piece, couple_dim)
        top = swapped(by_half[:h], couple_dim)
        bottom = swapped(by_couple[h:], half_dim)
        pieces += [piece, by_half, by_couple, top, bottom]
    added = placed_rows(jnp.concatenate(pieces, 0), root_targets, root_cols)
    root_rhs = root_source + row_sum(added, row_dims)

    chunks = max(2, min(ROOT_CHUNKS, root_rows // (4 * BLK)))
    unit = root_rows // chunks // 4
    share_width = nrhs // n_col
    partials, seconds = [], []
    for c in range(chunks):
        dims, weights = [half_dim, couple_dim], [1, 2]
        if c % 2 == 1:
            dims, weights = dims[::-1], weights[::-1]
        order = block_order(dims, c * 4, weights)
        partials.append((*panel_product(root_inverse, root_flags, root_rhs, order, unit), dims))
    for c in range(chunks):
        send, keep, dims = partials[c]
        came = swapped(send, dims[0])
        send, keep = keep[:unit] + came[:unit], keep[unit:] + came[unit:]
        seconds.append((keep, swapped(send, dims[1])))
    root_out = None
    for pair in range(chunks // 2):
        order = block_order(near_first, 0, [1 << bit for _, bit in near_first])
        send, keep = turned_sums(order, *seconds[2 * pair], *seconds[2 * pair + 1])
        for j, dim in enumerate(near_first):
            came = swapped(send, dim)
            if j == len(near_first) - 1:
                part = keep + came
            else:
                h = keep.shape[0] // 2
                send, keep = keep[:h] + came[:h], keep[h:] + came[h:]
        by_half = swapped(part, half_dim)
        by_couple = swapped(part, couple_dim)
        by_both = swapped(by_half, couple_dim)
        root_out = finished_rows(
            [part, by_half, by_couple, by_both], pair, leaf_index, root_rows, root_out
        )

    child_out = lax.dynamic_slice_in_dim(child_value, col_index * share_width, share_width, 1)
    middle_width = nrhs // 2 // n_col
    middle_out = lax.dynamic_slice_in_dim(
        middle_value, half * (nrhs // 2) + col_index * middle_width, middle_width, 1
    )
    return (child_out[None], middle_out[None], root_out.T)


def solution(mesh):
    placed = (
        P("leaf", "col", None),
        P("leaf", "col", None),
        P(("leaf", "col"), None),
        P("leaf", "row", "col"),
        P("leaf", "col", "row"),
        P("leaf", "row", "col"),
        P("leaf", "col", "row"),
        P("row", ("leaf", "col")),
        P("leaf", "row", "col"),
        P("leaf", "col", "row"),
        P("leaf", "row", "col"),
        P("leaf", "col", "row"),
        P("row", ("leaf", "col")),
        P(),
        P(),
    )
    return jax.shard_map(
        local,
        mesh=mesh,
        in_specs=placed,
        out_specs=(P("leaf", "row", "col"), P("leaf", "row", "col"), P("row", "col")),
        check_vma=False,
    )
```

```python
import functools

import jax
import jax.numpy as jnp
from jax import lax
from jax.experimental import pallas as pl
from jax.experimental.pallas import tpu as pltpu
from jax.sharding import PartitionSpec as P


BLK = 128
CHILD_CHUNKS = 4
MIDDLE_CHUNKS = 4
ROOT_CHUNKS = 8
CHILD_CALLS = (1, 3)
MIDDLE_CALLS = (1, 3)
ROOT_GATHERS = (2, 1, 1)
VMEM_BYTES = 56 * 2**20


def swapped(value, dim):
    axis, bit = dim
    pairs = [(source, source ^ (1 << bit)) for source in range(lax.axis_size(axis))]
    return lax.ppermute(value, axis, pairs)


def bit_of(dim):
    axis, bit = dim
    return (lax.axis_index(axis) >> bit) & 1


def bits_of(axis):
    return [(axis, bit) for bit in reversed(range(lax.axis_size(axis).bit_length() - 1))]


def block_order(dims, first, weights=None):
    n = len(dims)
    weights = weights or [1 << (n - 1 - j) for j in range(n)]
    mine = sum(bit_of(dim) * weight for dim, weight in zip(dims, weights, strict=True))
    order = []
    for place in range(1 << n):
        apart = sum(w for j, w in enumerate(weights) if not (place >> (n - 1 - j)) & 1)
        order.append(first + (mine ^ apart))
    return order


def exchange_stages(send, keep, dims):
    for j, dim in enumerate(dims):
        came = swapped(send, dim)
        if j == len(dims) - 1:
            value = keep + came
        else:
            h = keep.shape[0] // 2
            send, keep = keep[:h] + came[:h], keep[h:] + came[h:]
    for dim in reversed(dims):
        came = swapped(value, dim)
        value = jnp.concatenate([came, value], 0)
    return value


def reduce_scatter(send, keep, dims):
    for j, dim in enumerate(dims):
        came = swapped(send, dim)
        if j == len(dims) - 1:
            return keep + came
        h = keep.shape[0] // 2
        send, keep = keep[:h] + came[:h], keep[h:] + came[h:]
    return keep


def in_order(value, dims):
    shape = value.shape
    value = value.reshape((2,) * len(dims) + (-1,) + shape[1:])
    for j, dim in enumerate(dims):
        value = jnp.where(bit_of(dim) == 0, jnp.flip(value, j), value)
    return value.reshape(shape)


def split_into(target, value, width):
    high = value.astype(jnp.bfloat16)
    target[:, :width] = high
    target[:, width:] = (value - high.astype(jnp.float32)).astype(jnp.bfloat16)


def split_product(high, low, xs):
    width = xs.shape[1] // 2
    both = jnp.dot(high[...], xs[...], preferred_element_type=jnp.float32)
    rest = jnp.dot(low[...], xs[:, :width], preferred_element_type=jnp.float32)
    return both[:, :width] + (both[:, width:] + rest)


def panel_kernel(unit, merge, depth, cols_all, order, flags, *refs):
    panels, x, outs, (xs, high, low) = refs[:merge], refs[merge], refs[merge + 1 : -3], refs[-3:]
    width = x.shape[1]
    i = pl.program_id(0)

    @pl.when(i == 0)
    def _():
        split_into(xs, x[...], width)

    bs = min(unit, BLK)
    for u, panel in enumerate(panels):

        def put(b, carry, u=u, panel=panel):
            row_block = (order[i * merge + u] * unit + b * bs) // BLK
            rows = pl.ds(pl.multiple_of(b * bs, bs), bs)
            into = pl.ds(pl.multiple_of(u * unit + b * bs, bs), bs)
            for kb in range(depth // BLK):
                cols = slice(kb * BLK, (kb + 1) * BLK)
                flag = flags[row_block * cols_all + kb].astype(jnp.float32)
                kept = panel[rows, cols] * flag
                top = kept.astype(jnp.bfloat16)
                high[into, cols] = top
                low[into, cols] = (kept - top.astype(jnp.float32)).astype(jnp.bfloat16)
            return carry

        if unit // bs <= 4:
            for b in range(unit // bs):
                put(b, 0)
        else:
            lax.fori_loop(0, unit // bs, put, 0)
    result = split_product(high, low, xs)
    each = order.shape[0] // merge // len(outs)
    for at, out in enumerate(outs):

        @pl.when(i // each == at)
        def _(out=out):
            out[...] = result


def panel_product(panel, flags, x, orders, unit):
    depth, width = x.shape
    _, cols = panel.shape
    half = len(orders[0]) // 2
    merge = 1
    while merge * 2 <= half and merge * 2 * unit <= 512:
        merge *= 2
    steps = half // merge
    parts = 2 * len(orders)
    order = [block for some in orders for block in some]

    def place(part):
        return lambda i, order, flags: (jnp.clip(i - part * steps, 0, steps - 1), 0)

    def source(u):
        return lambda i, order, flags: (order[i * merge + u], 0)

    in_specs = [pl.BlockSpec((unit, depth), source(u)) for u in range(merge)]
    in_specs.append(pl.BlockSpec((depth, width), lambda i, order, flags: (0, 0)))
    n = len(order)
    outs = pl.pallas_call(
        functools.partial(panel_kernel, unit, merge, depth, cols // BLK),
        grid_spec=pltpu.PrefetchScalarGridSpec(
            num_scalar_prefetch=2,
            grid=(parts * steps,),
            in_specs=in_specs,
            out_specs=[pl.BlockSpec((merge * unit, width), place(part)) for part in range(parts)],
            scratch_shapes=[
                pltpu.VMEM((depth, 2 * width), jnp.bfloat16),
                pltpu.VMEM((merge * unit, depth), jnp.bfloat16),
                pltpu.VMEM((merge * unit, depth), jnp.bfloat16),
            ],
        ),
        out_shape=[jax.ShapeDtypeStruct((half * unit, width), jnp.float32)] * parts,
        compiler_params=pltpu.CompilerParams(vmem_limit_bytes=VMEM_BYTES),
        cost_estimate=pl.CostEstimate(
            flops=6 * n * unit * depth * width,
            bytes_accessed=4 * n * unit * (depth + width) + 4 * depth * width,
            transcendentals=0,
        ),
    )(jnp.stack(order).astype(jnp.int32), flags, *([panel] * merge), x)
    return [(outs[2 * c], outs[2 * c + 1]) for c in range(len(orders))]


def products_by_call(calls, chunks, panel, flags, x, orders, unit):
    if sum(calls) != chunks:
        calls = (1,) * chunks
    partials, first = [], 0
    for size in calls:
        partials += panel_product(panel, flags, x, orders[first : first + size], unit)
        first += size
    return partials


def update_kernel(unit, k_first, cols_all, n, count, with_acc, order, places, flags, *refs):
    panel, chunks, acc = refs[0], refs[1 : n + 1], refs[n + 1]
    out, xs, high, low, total = refs[-5:]
    rows, depth = panel.shape
    width = out.shape[1]
    i = pl.program_id(0)
    size = depth // count
    for c, chunk in enumerate(chunks):

        @pl.when(i == c)
        def _(c=c, chunk=chunk):
            def put(place, carry):
                there = pl.ds(pl.multiple_of(places[c * count + place] * size, size), size)
                value = chunk[pl.ds(pl.multiple_of(place * size, size), size), :]
                split_into(xs.at[there], value, width)
                return carry

            lax.fori_loop(0, count, put, 0)

    bs = min(rows, BLK)

    def split_band(b, carry):
        band = pl.ds(pl.multiple_of(b * bs, bs), bs)
        for kb in range(depth // BLK):
            cols = slice(kb * BLK, (kb + 1) * BLK)
            place = (b * bs // BLK) * cols_all + k_first + i * (depth // BLK) + kb
            kept = panel[band, cols] * flags[place].astype(jnp.float32)
            top = kept.astype(jnp.bfloat16)
            high[band, cols] = top
            low[band, cols] = (kept - top.astype(jnp.float32)).astype(jnp.bfloat16)
        return carry

    lax.fori_loop(0, rows // bs, split_band, 0)
    result = split_product(high, low, xs)

    @pl.when(i == 0)
    def _():
        total[...] = result

    @pl.when(i > 0)
    def _():
        total[...] += result

    @pl.when(i == pl.num_programs(0) - 1)
    def _():
        for j in range(rows // unit):
            there = pl.ds(pl.multiple_of(order[j] * unit, unit), unit)
            value = total[j * unit : (j + 1) * unit, :]
            if with_acc:
                value = value + acc[there, :]
            out[there, :] = value


def update_product(panel, flags, chunks, places, order, first, acc=None):
    depth, width = chunks[0].shape
    rows, cols = panel.shape
    n, count = len(chunks), len(places[0])
    whole = pl.BlockSpec((rows, width), lambda i, *_: (0, 0))
    in_specs = [pl.BlockSpec((rows, depth), lambda i, *_: (0, first + i))]
    in_specs += [pl.BlockSpec((depth, width), lambda i, *_: (0, 0))] * n
    args = [panel, *chunks]
    if acc is not None:
        in_specs.append(whole)
        args.append(acc)
    kernel = functools.partial(
        update_kernel, rows // len(order), first * (depth // BLK), cols // BLK, n, count, acc is not None
    )
    places = [place for some in places for place in some]
    return pl.pallas_call(
        kernel,
        grid_spec=pltpu.PrefetchScalarGridSpec(
            num_scalar_prefetch=3,
            grid=(n,),
            in_specs=in_specs,
            out_specs=whole,
            scratch_shapes=[
                pltpu.VMEM((depth, 2 * width), jnp.bfloat16),
                pltpu.VMEM((rows, depth), jnp.bfloat16),
                pltpu.VMEM((rows, depth), jnp.bfloat16),
                pltpu.VMEM((rows, width), jnp.float32),
            ],
        ),
        out_shape=jax.ShapeDtypeStruct((rows, width), jnp.float32),
        compiler_params=pltpu.CompilerParams(vmem_limit_bytes=VMEM_BYTES),
        cost_estimate=pl.CostEstimate(
            flops=6 * rows * n * depth * width,
            bytes_accessed=4 * (rows * n * depth + rows * width + n * depth * width),
            transcendentals=0,
        ),
    )(jnp.stack(order).astype(jnp.int32), jnp.stack(places).astype(jnp.int32), flags, *args)


def columns_kernel(n, count, window, places, first, *refs):
    chunks, (out, turned) = refs[:n], refs[n:]
    share, unit = out.shape[0], out.shape[1] // n // count
    start = jnp.minimum(first[0] // BLK, (chunks[0].shape[1] - window) // BLK) * BLK
    for c, chunk in enumerate(chunks):

        def put(place, carry, c=c, chunk=chunk):
            rows = pl.ds(pl.multiple_of(place * unit, unit), unit)
            there = (c * count + places[c * count + place]) * unit
            turned[...] = chunk[rows, pl.ds(pl.multiple_of(start, BLK), window)].T
            some = pl.ds(pl.multiple_of(first[0] - start, 8), share)
            out[:, pl.ds(pl.multiple_of(there, unit), unit)] = turned[some, :]
            return carry

        lax.fori_loop(0, count, put, 0)


def turned_columns(chunks, places, first, share):
    rows, width = chunks[0].shape
    n, count = len(chunks), len(places[0])
    window = min(width, 2 * BLK)
    whole = pl.BlockSpec((rows, width), lambda i, *_: (0, 0))
    places = [place for some in places for place in some]
    return pl.pallas_call(
        functools.partial(columns_kernel, n, count, window),
        grid_spec=pltpu.PrefetchScalarGridSpec(
            num_scalar_prefetch=2,
            grid=(1,),
            in_specs=[whole] * n,
            out_specs=pl.BlockSpec((share, n * rows), lambda i, *_: (0, 0)),
            scratch_shapes=[pltpu.VMEM((window, rows // count), jnp.float32)],
        ),
        out_shape=jax.ShapeDtypeStruct((share, n * rows), jnp.float32),
        compiler_params=pltpu.CompilerParams(vmem_limit_bytes=VMEM_BYTES),
        cost_estimate=pl.CostEstimate(
            flops=0, bytes_accessed=4 * n * rows * (width + share), transcendentals=0
        ),
    )(
        jnp.stack(places).astype(jnp.int32),
        jnp.reshape(first, (1,)).astype(jnp.int32),
        *chunks,
    )


def turn_kernel(order, *refs):
    parts, (send, keep, whole) = refs[:-3], refs[-3:]
    h = parts[0].shape[0]
    each = len(parts) // 2
    for at in range(2):
        value = parts[at * each][...]
        for part in parts[at * each + 1 : (at + 1) * each]:
            value = value + part[...]
        whole[:, at * h : (at + 1) * h] = value.T
    count = order.shape[0]
    share = whole.shape[0] // count
    for place in range(count):
        out = send if place < count // 2 else keep
        at = place % (count // 2) * share
        out[at : at + share, :] = whole[pl.ds(pl.multiple_of(order[place] * share, share), share), :]


def turned_sums(order, *parts):
    rows, width = parts[0].shape
    whole = pl.BlockSpec((rows, width), lambda i, order: (0, 0))
    half = pl.BlockSpec((width // 2, 2 * rows), lambda i, order: (0, 0))
    return pl.pallas_call(
        turn_kernel,
        grid_spec=pltpu.PrefetchScalarGridSpec(
            num_scalar_prefetch=1,
            grid=(1,),
            in_specs=[whole] * len(parts),
            out_specs=[half, half],
            scratch_shapes=[pltpu.VMEM((width, 2 * rows), jnp.float32)],
        ),
        out_shape=[jax.ShapeDtypeStruct((width // 2, 2 * rows), jnp.float32)] * 2,
        compiler_params=pltpu.CompilerParams(vmem_limit_bytes=VMEM_BYTES),
        cost_estimate=pl.CostEstimate(
            flops=2 * rows * width,
            bytes_accessed=4 * (len(parts) + 2) * rows * width,
            transcendentals=0,
        ),
    )(jnp.stack(order).astype(jnp.int32), *parts)


def finish_kernel(pairs, unit, leaf, *refs):
    pieces, (out, sems) = refs[:4], refs[-2:]
    copies = []
    for k, piece in enumerate(pieces):
        for at, pair in enumerate(pairs):
            for h in range(1 if pair == 0 else 2):
                size = 2 * unit if pair == 0 else unit
                first = ((2 * pair + h) * 4 * unit) + (leaf[0] ^ k) * size
                there = pl.ds(pl.multiple_of(first, unit), size)
                here = slice((2 * at + h) * unit, (2 * at + h) * unit + size)
                copies.append(
                    pltpu.make_async_copy(piece.at[:, here], out.at[:, there], sems.at[len(copies)])
                )
    for copy in copies:
        copy.start()
    for copy in copies:
        copy.wait()


def finished_rows(pieces, pairs, leaf_index, rows, before):
    width, both = pieces[0].shape
    unit = both // 2 // len(pairs)
    whole = pl.BlockSpec((width, both), lambda i, leaf: (0, 0))
    in_specs, args = [whole] * 4, list(pieces)
    aliases = {}
    if before is not None:
        in_specs.append(pl.BlockSpec(memory_space=pl.ANY))
        args.append(before)
        aliases = {5: 0}
    return pl.pallas_call(
        functools.partial(finish_kernel, pairs, unit),
        grid_spec=pltpu.PrefetchScalarGridSpec(
            num_scalar_prefetch=1,
            grid=(1,),
            in_specs=in_specs,
            out_specs=pl.BlockSpec(memory_space=pl.ANY),
            scratch_shapes=[pltpu.SemaphoreType.DMA((8 * len(pairs),))],
        ),
        out_shape=jax.ShapeDtypeStruct((width, rows), jnp.float32),
        input_output_aliases=aliases,
        compiler_params=pltpu.CompilerParams(vmem_limit_bytes=VMEM_BYTES),
        cost_estimate=pl.CostEstimate(
            flops=0, bytes_accessed=64 * unit * width * len(pairs), transcendentals=0
        ),
    )(jnp.reshape(leaf_index, (1,)).astype(jnp.int32), *args)


def place_kernel(n, with_acc, targets, *refs):
    pieces, (out, total, split) = refs[:n], refs[-3:]
    width = out.shape[1]
    first = 0
    for piece in pieces:
        rows = piece.shape[0]
        split_into(split.at[first : first + rows], piece[...], width)
        first += rows
    tiles, _, tile = targets.shape
    row_ids = lax.broadcasted_iota(jnp.int32, (out.shape[0], tile), 0)
    total[...] = jnp.zeros_like(total)

    def step(t, carry):
        hits = jnp.where(row_ids == targets[t], 1.0, 0.0).astype(jnp.bfloat16)
        these = split[pl.ds(pl.multiple_of(t * tile, tile), tile), :]
        total[...] += jnp.dot(hits, these, preferred_element_type=jnp.float32)
        return carry

    lax.fori_loop(0, tiles, step, 0)
    value = total[:, :width] + total[:, width:]
    out[...] = value + refs[n][...] if with_acc else value


def placed_rows(pieces, targets, count, acc=None):
    total = sum(piece.shape[0] for piece in pieces)
    width = pieces[0].shape[1]
    tile = min(total, 1024)
    args = [targets.reshape(total // tile, 1, tile), *pieces]
    if acc is not None:
        args.append(acc)
    return pl.pallas_call(
        functools.partial(place_kernel, len(pieces), acc is not None),
        out_shape=jax.ShapeDtypeStruct((count, width), jnp.float32),
        scratch_shapes=[
            pltpu.VMEM((count, 2 * width), jnp.float32),
            pltpu.VMEM((total, 2 * width), jnp.bfloat16),
        ],
        compiler_params=pltpu.CompilerParams(vmem_limit_bytes=VMEM_BYTES),
        cost_estimate=pl.CostEstimate(
            flops=4 * total * count * width, bytes_accessed=4 * width * (total + count), transcendentals=0
        ),
    )(*args)


def placed_pieces(lines, targets, count, cuts):
    rows = sum(part.shape[0] for part in lines[0])
    added = None
    edges = [0, *cuts, len(lines)]
    for low, high in zip(edges[:-1], edges[1:], strict=True):
        some = [part for parts in lines[low:high] for part in parts]
        added = placed_rows(some, targets[low * rows : high * rows], count, added)
    return added


def lower_flags(pattern, row_first, col_first):
    rows, cols = pattern.shape
    row_ids = row_first + jnp.arange(rows, dtype=jnp.int32)[:, None]
    col_ids = col_first + jnp.arange(cols, dtype=jnp.int32)[None, :]
    keep = (row_ids == col_ids) | (row_ids > col_ids) & (pattern == 1)
    return keep.astype(jnp.int32).reshape(-1)


def gather_line(own, dims):
    pieces = {0: own}
    for axis, bit in dims:
        for k in list(pieces):
            pieces[k ^ (1 << bit)] = swapped(pieces[k], (axis, bit))
    return [pieces[k] for k in range(len(pieces))]


def relative(table, axis, dim):
    for bit in range(table.shape[axis].bit_length() - 1):
        shape = table.shape
        cut = shape[:axis] + (shape[axis] >> (bit + 1), 2, 1 << bit) + shape[axis + 1 :]
        parts = table.reshape(cut)
        own = (dim >> bit) & 1
        table = jnp.where(own == 1, jnp.flip(parts, axis + 1), parts).reshape(shape)
    return table


def row_sum(value, row_dims):
    for dim in row_dims:
        value = value + swapped(value, dim)
    return value


def local(
    child_source,
    middle_source,
    root_source,
    child_inverse,
    child_update,
    middle_inverse,
    middle_update,
    root_inverse,
    child_diagmask,
    child_updmask,
    middle_diagmask,
    middle_updmask,
    root_diagmask,
    child_rowmap,
    middle_rowmap,
):
    leaf_index = lax.axis_index("leaf")
    row_index = lax.axis_index("row")
    col_index = lax.axis_index("col")
    n_leaf = lax.axis_size("leaf")
    n_row = lax.axis_size("row")
    n_col = lax.axis_size("col")
    half = leaf_index % 2
    couple = leaf_index // 2
    nrhs = child_source.shape[2]
    half_dim, couple_dim = ("leaf", 0), ("leaf", 1)
    row_dims = bits_of("row")
    col_dims = bits_of("col")
    near_first = list(reversed(col_dims))

    child_rows, child_cols = child_inverse.shape[1:]
    middle_rows, middle_cols = middle_inverse.shape[1:]
    root_rows, root_cols = root_inverse.shape
    middle_first = (half * n_col + col_index) * middle_cols
    root_first = (leaf_index * n_col + col_index) * root_cols

    child_flags = lower_flags(
        child_diagmask[0], row_index * (child_rows // BLK), col_index * (child_cols // BLK)
    )
    middle_flags = lower_flags(
        middle_diagmask[0], row_index * (middle_rows // BLK), middle_first // BLK
    )
    root_flags = lower_flags(root_diagmask, row_index * (root_rows // BLK), root_first // BLK)
    child_upd_flags = child_updmask[0].reshape(-1)
    middle_upd_flags = middle_updmask[0].reshape(-1)

    child_lift_rows = child_update.shape[1]
    middle_lift_rows = middle_update.shape[1]
    pair_targets = lax.dynamic_slice_in_dim(child_rowmap, 2 * couple, 2, 0)
    pair_targets = pair_targets.reshape(2, n_col, n_row, child_lift_rows // n_row)
    pair_targets = lax.dynamic_index_in_dim(pair_targets, row_index, 2, False)
    pair_targets = relative(relative(pair_targets, 0, half), 1, col_index)
    pair_targets = pair_targets.transpose(1, 0, 2).reshape(-1) - middle_first
    root_targets = middle_rowmap.reshape(n_leaf, n_col, n_row, middle_lift_rows // n_row)
    root_targets = lax.dynamic_index_in_dim(root_targets, row_index, 2, False)
    root_targets = relative(relative(root_targets, 0, leaf_index), 1, col_index)
    root_targets = root_targets.transpose(1, 0, 2).reshape(-1) - root_first

    def chunked(panel, flags, x, plans, chunks, calls, update, update_flags):
        rows = panel.shape[0]
        count = 1 << len(plans[0])
        chunks = max(1, min(chunks, rows // (count * BLK)))
        unit = rows // chunks // count
        lift_order = block_order(row_dims, 0)
        plans = [plans[min(c, len(plans) - 1)] for c in range(chunks)]
        orders = [block_order(plans[c], c * count) for c in range(chunks)]
        partials = products_by_call(calls, chunks, panel, flags, x, orders, unit)
        values = [exchange_stages(*partials[c], plans[c]) for c in range(chunks)]
        places = [block_order(plans[c], 0) for c in range(chunks)]
        lift = None
        if chunks > 1:
            lift = update_product(
                update, update_flags, values[:-1], places[:-1], lift_order, 0
            )
        lift = update_product(
            update, update_flags, values[-1:], places[-1:], lift_order, chunks - 1, lift
        )

        def columns(first, width):
            if unit % BLK == 0:
                return turned_columns(values, places, first, width).T
            parts = [lax.dynamic_slice_in_dim(value, first, width, 1) for value in values]
            return jnp.concatenate(
                [in_order(part, plan) for part, plan in zip(parts, plans, strict=True)], 0
            )

        h = lift.shape[0] // 2
        return columns, reduce_scatter(lift[:h], lift[h:], row_dims)

    child_columns, child_lift = chunked(
        child_inverse[0], child_flags, child_source[0], [near_first], CHILD_CHUNKS, CHILD_CALLS,
        child_update[0], child_upd_flags,
    )
    pieces = []
    for piece in gather_line(child_lift, col_dims):
        pieces.append([piece, swapped(piece, half_dim)])
    added = placed_pieces(pieces, pair_targets, middle_cols, [])
    middle_rhs = middle_source[0] + row_sum(added, row_dims)

    middle_columns, middle_lift = chunked(
        middle_inverse[0], middle_flags, middle_rhs, [[half_dim] + near_first],
        MIDDLE_CHUNKS, MIDDLE_CALLS,
        middle_update[0], middle_upd_flags,
    )
    pieces = []
    for piece in gather_line(middle_lift, col_dims):
        h = piece.shape[0] // 2
        by_half = swapped(piece, half_dim)
        by_couple = swapped(piece, couple_dim)
        top = swapped(by_half[:h], couple_dim)
        bottom = swapped(by_couple[h:], half_dim)
        pieces.append([piece, by_half, by_couple, top, bottom])
    added = placed_pieces(pieces, root_targets, root_cols, [])
    root_rhs = root_source + row_sum(added, row_dims)

    chunks = max(2, min(ROOT_CHUNKS, root_rows // (4 * BLK)))
    unit = root_rows // chunks // 4
    share_width = nrhs // n_col
    pairs_count = chunks // 2
    col_order = block_order(near_first, 0, [1 << bit for _, bit in near_first])
    plans = [([half_dim, couple_dim], [1, 2]), ([couple_dim, half_dim], [2, 1])]

    def product_of(pair):
        size = 2 * unit if pair == 0 else unit
        orders = [block_order(plans[0][0], 0, plans[0][1])]
        if pair > 0:
            orders = [block_order(*plans[h][:1], (2 * pair + h) * 4, plans[h][1]) for h in range(2)]
        return panel_product(root_inverse, root_flags, root_rhs, orders, size)

    def col_sums(send, keep):
        for j, dim in enumerate(near_first):
            came = swapped(send, dim)
            if j < len(near_first) - 1:
                h = keep.shape[0] // 2
                send, keep = keep[:h] + came[:h], keep[h:] + came[h:]
        return keep, came

    order_of_pairs = range(pairs_count)
    products = {pair: product_of(pair) for pair in order_of_pairs}
    sums = []
    for pair in range(pairs_count):
        if pair == 0:
            send, keep = turned_sums(col_order, *products[0][0])
            keep, came = col_sums(send, keep)
            h = keep.shape[1] // 2
            send, keep = keep[:, :h] + came[:, :h], keep[:, h:] + came[:, h:]
            came = swapped(send, half_dim)
            h //= 2
            send, keep = keep[:, :h] + came[:, :h], keep[:, h:] + came[:, h:]
            came = swapped(send, couple_dim)
            sums.append(keep + came)
            continue
        seconds = []
        for h in range(2):
            (send, keep), (dims, _) = products[pair][h], plans[h]
            came = swapped(send, dims[0])
            send, keep = keep[:unit] + came[:unit], keep[unit:] + came[unit:]
            seconds += [keep, swapped(send, dims[1])]
        send, keep = turned_sums(col_order, *seconds)
        keep, came = col_sums(send, keep)
        sums.append(keep + came)
    gathers = ROOT_GATHERS if sum(ROOT_GATHERS) == pairs_count else (1,) * pairs_count
    root_out, first = None, 0
    for g, size in enumerate(gathers):
        pairs = range(first, first + size)
        first += size
        part = jnp.concatenate([sums[pair] for pair in pairs], 1)
        by_half = swapped(part, half_dim)
        by_couple = swapped(part, couple_dim)
        by_both = swapped(by_half, couple_dim) if g % 2 == 0 else swapped(by_couple, half_dim)
        root_out = finished_rows(
            [part, by_half, by_couple, by_both], pairs, leaf_index, root_rows, root_out
        )

    child_out = child_columns(col_index * share_width, share_width)
    middle_width = nrhs // 2 // n_col
    middle_out = middle_columns(half * (nrhs // 2) + col_index * middle_width, middle_width)
    return (child_out[None], middle_out[None], root_out.T)


def solution(mesh):
    placed = (
        P("leaf", "col", None),
        P("leaf", "col", None),
        P(("leaf", "col"), None),
        P("leaf", "row", "col"),
        P("leaf", "col", "row"),
        P("leaf", "row", "col"),
        P("leaf", "col", "row"),
        P("row", ("leaf", "col")),
        P("leaf", "row", "col"),
        P("leaf", "col", "row"),
        P("leaf", "row", "col"),
        P("leaf", "col", "row"),
        P("row", ("leaf", "col")),
        P(),
        P(),
    )
    return jax.shard_map(
        local,
        mesh=mesh,
        in_specs=placed,
        out_specs=(P("leaf", "row", "col"), P("leaf", "row", "col"), P("row", "col")),
        check_vma=False,
    )
```

```python
import functools

import jax
import jax.numpy as jnp
from jax import lax
from jax.experimental import pallas as pl
from jax.experimental.pallas import tpu as pltpu
from jax.sharding import PartitionSpec as P


BLK = 128
CHILD_CHUNKS = 4
MIDDLE_CHUNKS = 4
ROOT_CHUNKS = 8
CHILD_CALLS = (1, 3)
MIDDLE_CALLS = (1, 3)
ROOT_GATHERS = (2, 1, 1)
VMEM_BYTES = 56 * 2**20


def swapped(value, dim):
    axis, bit = dim
    pairs = [(source, source ^ (1 << bit)) for source in range(lax.axis_size(axis))]
    return lax.ppermute(value, axis, pairs)


def bit_of(dim):
    axis, bit = dim
    return (lax.axis_index(axis) >> bit) & 1


def bits_of(axis):
    return [(axis, bit) for bit in reversed(range(lax.axis_size(axis).bit_length() - 1))]


def block_order(dims, first, weights=None):
    n = len(dims)
    weights = weights or [1 << (n - 1 - j) for j in range(n)]
    mine = sum(bit_of(dim) * weight for dim, weight in zip(dims, weights, strict=True))
    order = []
    for place in range(1 << n):
        apart = sum(w for j, w in enumerate(weights) if not (place >> (n - 1 - j)) & 1)
        order.append(first + (mine ^ apart))
    return order


def exchange_stages(send, keep, dims):
    for j, dim in enumerate(dims):
        came = swapped(send, dim)
        if j == len(dims) - 1:
            value = keep + came
        else:
            h = keep.shape[0] // 2
            send, keep = keep[:h] + came[:h], keep[h:] + came[h:]
    for dim in reversed(dims):
        came = swapped(value, dim)
        value = jnp.concatenate([came, value], 0)
    return value


def reduce_scatter(send, keep, dims):
    for j, dim in enumerate(dims):
        came = swapped(send, dim)
        if j == len(dims) - 1:
            return keep + came
        h = keep.shape[0] // 2
        send, keep = keep[:h] + came[:h], keep[h:] + came[h:]
    return keep


def in_order(value, dims):
    shape = value.shape
    value = value.reshape((2,) * len(dims) + (-1,) + shape[1:])
    for j, dim in enumerate(dims):
        value = jnp.where(bit_of(dim) == 0, jnp.flip(value, j), value)
    return value.reshape(shape)


def split_into(target, value, width):
    high = value.astype(jnp.bfloat16)
    target[:, :width] = high
    target[:, width:] = (value - high.astype(jnp.float32)).astype(jnp.bfloat16)


def split_product(high, low, xs):
    width = xs.shape[1] // 2
    both = jnp.dot(high[...], xs[...], preferred_element_type=jnp.float32)
    rest = jnp.dot(low[...], xs[:, :width], preferred_element_type=jnp.float32)
    return both[:, :width] + (both[:, width:] + rest)


def panel_kernel(unit, merge, depth, cols_all, order, flags, *refs):
    panels, x, outs, (xs, high, low) = refs[:merge], refs[merge], refs[merge + 1 : -3], refs[-3:]
    width = x.shape[1]
    i = pl.program_id(0)

    @pl.when(i == 0)
    def _():
        split_into(xs, x[...], width)

    bs = min(unit, BLK)
    for u, panel in enumerate(panels):

        def put(b, carry, u=u, panel=panel):
            row_block = (order[i * merge + u] * unit + b * bs) // BLK
            rows = pl.ds(pl.multiple_of(b * bs, bs), bs)
            into = pl.ds(pl.multiple_of(u * unit + b * bs, bs), bs)
            for kb in range(depth // BLK):
                cols = slice(kb * BLK, (kb + 1) * BLK)
                flag = flags[row_block * cols_all + kb].astype(jnp.float32)
                kept = panel[rows, cols] * flag
                top = kept.astype(jnp.bfloat16)
                high[into, cols] = top
                low[into, cols] = (kept - top.astype(jnp.float32)).astype(jnp.bfloat16)
            return carry

        if unit // bs <= 4:
            for b in range(unit // bs):
                put(b, 0)
        else:
            lax.fori_loop(0, unit // bs, put, 0)
    result = split_product(high, low, xs)
    each = order.shape[0] // merge // len(outs)
    for at, out in enumerate(outs):

        @pl.when(i // each == at)
        def _(out=out):
            out[...] = result


def panel_product(panel, flags, x, orders, unit):
    depth, width = x.shape
    _, cols = panel.shape
    half = len(orders[0]) // 2
    merge = 1
    while merge * 2 <= half and merge * 2 * unit <= 512:
        merge *= 2
    steps = half // merge
    parts = 2 * len(orders)
    order = [block for some in orders for block in some]

    def place(part):
        return lambda i, order, flags: (jnp.clip(i - part * steps, 0, steps - 1), 0)

    def source(u):
        return lambda i, order, flags: (order[i * merge + u], 0)

    in_specs = [pl.BlockSpec((unit, depth), source(u)) for u in range(merge)]
    in_specs.append(pl.BlockSpec((depth, width), lambda i, order, flags: (0, 0)))
    n = len(order)
    outs = pl.pallas_call(
        functools.partial(panel_kernel, unit, merge, depth, cols // BLK),
        grid_spec=pltpu.PrefetchScalarGridSpec(
            num_scalar_prefetch=2,
            grid=(parts * steps,),
            in_specs=in_specs,
            out_specs=[pl.BlockSpec((merge * unit, width), place(part)) for part in range(parts)],
            scratch_shapes=[
                pltpu.VMEM((depth, 2 * width), jnp.bfloat16),
                pltpu.VMEM((merge * unit, depth), jnp.bfloat16),
                pltpu.VMEM((merge * unit, depth), jnp.bfloat16),
            ],
        ),
        out_shape=[jax.ShapeDtypeStruct((half * unit, width), jnp.float32)] * parts,
        compiler_params=pltpu.CompilerParams(vmem_limit_bytes=VMEM_BYTES),
        cost_estimate=pl.CostEstimate(
            flops=6 * n * unit * depth * width,
            bytes_accessed=4 * n * unit * (depth + width) + 4 * depth * width,
            transcendentals=0,
        ),
    )(jnp.stack(order).astype(jnp.int32), flags, *([panel] * merge), x)
    return [(outs[2 * c], outs[2 * c + 1]) for c in range(len(orders))]


def products_by_call(calls, chunks, panel, flags, x, orders, unit):
    if sum(calls) != chunks:
        calls = (1,) * chunks
    partials, first = [], 0
    for size in calls:
        partials += panel_product(panel, flags, x, orders[first : first + size], unit)
        first += size
    return partials


def update_kernel(unit, k_first, cols_all, n, count, with_acc, order, places, flags, *refs):
    panel, chunks, acc = refs[0], refs[1 : n + 1], refs[n + 1]
    out, xs, high, low, total = refs[-5:]
    rows, depth = panel.shape
    width = out.shape[1]
    i = pl.program_id(0)
    size = depth // count
    for c, chunk in enumerate(chunks):

        @pl.when(i == c)
        def _(c=c, chunk=chunk):
            def put(place, carry):
                there = pl.ds(pl.multiple_of(places[c * count + place] * size, size), size)
                value = chunk[pl.ds(pl.multiple_of(place * size, size), size), :]
                split_into(xs.at[there], value, width)
                return carry

            lax.fori_loop(0, count, put, 0)

    bs = min(rows, BLK)

    def split_band(b, carry):
        band = pl.ds(pl.multiple_of(b * bs, bs), bs)
        for kb in range(depth // BLK):
            cols = slice(kb * BLK, (kb + 1) * BLK)
            place = (b * bs // BLK) * cols_all + k_first + i * (depth // BLK) + kb
            kept = panel[band, cols] * flags[place].astype(jnp.float32)
            top = kept.astype(jnp.bfloat16)
            high[band, cols] = top
            low[band, cols] = (kept - top.astype(jnp.float32)).astype(jnp.bfloat16)
        return carry

    lax.fori_loop(0, rows // bs, split_band, 0)
    result = split_product(high, low, xs)

    @pl.when(i == 0)
    def _():
        total[...] = result

    @pl.when(i > 0)
    def _():
        total[...] += result

    @pl.when(i == pl.num_programs(0) - 1)
    def _():
        for j in range(rows // unit):
            there = pl.ds(pl.multiple_of(order[j] * unit, unit), unit)
            value = total[j * unit : (j + 1) * unit, :]
            if with_acc:
                value = value + acc[there, :]
            out[there, :] = value


def update_product(panel, flags, chunks, places, order, first, acc=None):
    depth, width = chunks[0].shape
    rows, cols = panel.shape
    n, count = len(chunks), len(places[0])
    whole = pl.BlockSpec((rows, width), lambda i, *_: (0, 0))
    in_specs = [pl.BlockSpec((rows, depth), lambda i, *_: (0, first + i))]
    in_specs += [pl.BlockSpec((depth, width), lambda i, *_: (0, 0))] * n
    args = [panel, *chunks]
    if acc is not None:
        in_specs.append(whole)
        args.append(acc)
    kernel = functools.partial(
        update_kernel, rows // len(order), first * (depth // BLK), cols // BLK, n, count, acc is not None
    )
    places = [place for some in places for place in some]
    return pl.pallas_call(
        kernel,
        grid_spec=pltpu.PrefetchScalarGridSpec(
            num_scalar_prefetch=3,
            grid=(n,),
            in_specs=in_specs,
            out_specs=whole,
            scratch_shapes=[
                pltpu.VMEM((depth, 2 * width), jnp.bfloat16),
                pltpu.VMEM((rows, depth), jnp.bfloat16),
                pltpu.VMEM((rows, depth), jnp.bfloat16),
                pltpu.VMEM((rows, width), jnp.float32),
            ],
        ),
        out_shape=jax.ShapeDtypeStruct((rows, width), jnp.float32),
        compiler_params=pltpu.CompilerParams(vmem_limit_bytes=VMEM_BYTES),
        cost_estimate=pl.CostEstimate(
            flops=6 * rows * n * depth * width,
            bytes_accessed=4 * (rows * n * depth + rows * width + n * depth * width),
            transcendentals=0,
        ),
    )(jnp.stack(order).astype(jnp.int32), jnp.stack(places).astype(jnp.int32), flags, *args)


def columns_kernel(n, count, window, places, first, *refs):
    chunks, (out, turned) = refs[:n], refs[n:]
    share, unit = out.shape[0], out.shape[1] // n // count
    start = jnp.minimum(first[0] // BLK, (chunks[0].shape[1] - window) // BLK) * BLK
    for c, chunk in enumerate(chunks):

        def put(place, carry, c=c, chunk=chunk):
            rows = pl.ds(pl.multiple_of(place * unit, unit), unit)
            there = (c * count + places[c * count + place]) * unit
            turned[...] = chunk[rows, pl.ds(pl.multiple_of(start, BLK), window)].T
            some = pl.ds(pl.multiple_of(first[0] - start, 8), share)
            out[:, pl.ds(pl.multiple_of(there, unit), unit)] = turned[some, :]
            return carry

        lax.fori_loop(0, count, put, 0)


def turned_columns(chunks, places, first, share):
    rows, width = chunks[0].shape
    n, count = len(chunks), len(places[0])
    window = min(width, 2 * BLK)
    whole = pl.BlockSpec((rows, width), lambda i, *_: (0, 0))
    places = [place for some in places for place in some]
    return pl.pallas_call(
        functools.partial(columns_kernel, n, count, window),
        grid_spec=pltpu.PrefetchScalarGridSpec(
            num_scalar_prefetch=2,
            grid=(1,),
            in_specs=[whole] * n,
            out_specs=pl.BlockSpec((share, n * rows), lambda i, *_: (0, 0)),
            scratch_shapes=[pltpu.VMEM((window, rows // count), jnp.float32)],
        ),
        out_shape=jax.ShapeDtypeStruct((share, n * rows), jnp.float32),
        compiler_params=pltpu.CompilerParams(vmem_limit_bytes=VMEM_BYTES),
        cost_estimate=pl.CostEstimate(
            flops=0, bytes_accessed=4 * n * rows * (width + share), transcendentals=0
        ),
    )(
        jnp.stack(places).astype(jnp.int32),
        jnp.reshape(first, (1,)).astype(jnp.int32),
        *chunks,
    )


def turn_kernel(order, *refs):
    parts, (send, keep, whole) = refs[:-3], refs[-3:]
    h = parts[0].shape[0]
    each = len(parts) // 2
    for at in range(2):
        value = parts[at * each][...]
        for part in parts[at * each + 1 : (at + 1) * each]:
            value = value + part[...]
        whole[:, at * h : (at + 1) * h] = value.T
    count = order.shape[0]
    share = whole.shape[0] // count
    for place in range(count):
        out = send if place < count // 2 else keep
        at = place % (count // 2) * share
        out[at : at + share, :] = whole[pl.ds(pl.multiple_of(order[place] * share, share), share), :]


def turned_sums(order, *parts):
    rows, width = parts[0].shape
    whole = pl.BlockSpec((rows, width), lambda i, order: (0, 0))
    half = pl.BlockSpec((width // 2, 2 * rows), lambda i, order: (0, 0))
    return pl.pallas_call(
        turn_kernel,
        grid_spec=pltpu.PrefetchScalarGridSpec(
            num_scalar_prefetch=1,
            grid=(1,),
            in_specs=[whole] * len(parts),
            out_specs=[half, half],
            scratch_shapes=[pltpu.VMEM((width, 2 * rows), jnp.float32)],
        ),
        out_shape=[jax.ShapeDtypeStruct((width // 2, 2 * rows), jnp.float32)] * 2,
        compiler_params=pltpu.CompilerParams(vmem_limit_bytes=VMEM_BYTES),
        cost_estimate=pl.CostEstimate(
            flops=2 * rows * width,
            bytes_accessed=4 * (len(parts) + 2) * rows * width,
            transcendentals=0,
        ),
    )(jnp.stack(order).astype(jnp.int32), *parts)


def finish_kernel(groups, unit, leaf, *refs):
    pieces, (out, sems) = refs[: 4 * len(groups)], refs[-2:]
    copies = []
    for g, pairs in enumerate(groups):
        for k, piece in enumerate(pieces[4 * g : 4 * g + 4]):
            for at, pair in enumerate(pairs):
                for h in range(1 if pair == 0 else 2):
                    size = 2 * unit if pair == 0 else unit
                    first = ((2 * pair + h) * 4 * unit) + (leaf[0] ^ k) * size
                    there = pl.ds(pl.multiple_of(first, unit), size)
                    here = slice((2 * at + h) * unit, (2 * at + h) * unit + size)
                    copies.append(
                        pltpu.make_async_copy(
                            piece.at[:, here], out.at[:, there], sems.at[len(copies)]
                        )
                    )
    for copy in copies:
        copy.start()
    for copy in copies:
        copy.wait()


def finished_rows(pieces, groups, leaf_index, rows, before):
    width, both = pieces[0].shape
    unit = both // 2 // len(groups[0])
    in_specs = [pl.BlockSpec(piece.shape, lambda i, leaf: (0, 0)) for piece in pieces]
    args = list(pieces)
    aliases = {}
    if before is not None:
        in_specs.append(pl.BlockSpec(memory_space=pl.ANY))
        args.append(before)
        aliases = {1 + len(pieces): 0}
    count = sum(len(pairs) for pairs in groups)
    return pl.pallas_call(
        functools.partial(finish_kernel, groups, unit),
        grid_spec=pltpu.PrefetchScalarGridSpec(
            num_scalar_prefetch=1,
            grid=(1,),
            in_specs=in_specs,
            out_specs=pl.BlockSpec(memory_space=pl.ANY),
            scratch_shapes=[pltpu.SemaphoreType.DMA((8 * count,))],
        ),
        out_shape=jax.ShapeDtypeStruct((width, rows), jnp.float32),
        input_output_aliases=aliases,
        compiler_params=pltpu.CompilerParams(vmem_limit_bytes=VMEM_BYTES),
        cost_estimate=pl.CostEstimate(
            flops=0, bytes_accessed=64 * unit * width * count, transcendentals=0
        ),
    )(jnp.reshape(leaf_index, (1,)).astype(jnp.int32), *args)


def place_kernel(n, with_acc, targets, *refs):
    pieces, (out, total, split) = refs[:n], refs[-3:]
    width = out.shape[1]
    first = 0
    for piece in pieces:
        rows = piece.shape[0]
        split_into(split.at[first : first + rows], piece[...], width)
        first += rows
    tiles, _, tile = targets.shape
    row_ids = lax.broadcasted_iota(jnp.int32, (out.shape[0], tile), 0)
    total[...] = jnp.zeros_like(total)

    def step(t, carry):
        hits = jnp.where(row_ids == targets[t], 1.0, 0.0).astype(jnp.bfloat16)
        these = split[pl.ds(pl.multiple_of(t * tile, tile), tile), :]
        total[...] += jnp.dot(hits, these, preferred_element_type=jnp.float32)
        return carry

    lax.fori_loop(0, tiles, step, 0)
    value = total[:, :width] + total[:, width:]
    out[...] = value + refs[n][...] if with_acc else value


def placed_rows(pieces, targets, count, acc=None):
    total = sum(piece.shape[0] for piece in pieces)
    width = pieces[0].shape[1]
    tile = min(total, 512)
    args = [targets.reshape(total // tile, 1, tile), *pieces]
    if acc is not None:
        args.append(acc)
    return pl.pallas_call(
        functools.partial(place_kernel, len(pieces), acc is not None),
        out_shape=jax.ShapeDtypeStruct((count, width), jnp.float32),
        scratch_shapes=[
            pltpu.VMEM((count, 2 * width), jnp.float32),
            pltpu.VMEM((total, 2 * width), jnp.bfloat16),
        ],
        compiler_params=pltpu.CompilerParams(vmem_limit_bytes=VMEM_BYTES),
        cost_estimate=pl.CostEstimate(
            flops=4 * total * count * width, bytes_accessed=4 * width * (total + count), transcendentals=0
        ),
    )(*args)


def placed_pieces(lines, targets, count, cuts):
    rows = sum(part.shape[0] for part in lines[0])
    added = None
    edges = [0, *cuts, len(lines)]
    for low, high in zip(edges[:-1], edges[1:], strict=True):
        some = [part for parts in lines[low:high] for part in parts]
        added = placed_rows(some, targets[low * rows : high * rows], count, added)
    return added


def lower_flags(pattern, row_first, col_first):
    rows, cols = pattern.shape
    row_ids = row_first + jnp.arange(rows, dtype=jnp.int32)[:, None]
    col_ids = col_first + jnp.arange(cols, dtype=jnp.int32)[None, :]
    keep = (row_ids == col_ids) | (row_ids > col_ids) & (pattern == 1)
    return keep.astype(jnp.int32).reshape(-1)


def gather_line(own, dims):
    pieces = {0: own}
    for axis, bit in dims:
        for k in list(pieces):
            pieces[k ^ (1 << bit)] = swapped(pieces[k], (axis, bit))
    return [pieces[k] for k in range(len(pieces))]


def relative(table, axis, dim):
    for bit in range(table.shape[axis].bit_length() - 1):
        shape = table.shape
        cut = shape[:axis] + (shape[axis] >> (bit + 1), 2, 1 << bit) + shape[axis + 1 :]
        parts = table.reshape(cut)
        own = (dim >> bit) & 1
        table = jnp.where(own == 1, jnp.flip(parts, axis + 1), parts).reshape(shape)
    return table


def row_sum(value, row_dims):
    for dim in row_dims:
        value = value + swapped(value, dim)
    return value


def local(
    child_source,
    middle_source,
    root_source,
    child_inverse,
    child_update,
    middle_inverse,
    middle_update,
    root_inverse,
    child_diagmask,
    child_updmask,
    middle_diagmask,
    middle_updmask,
    root_diagmask,
    child_rowmap,
    middle_rowmap,
):
    leaf_index = lax.axis_index("leaf")
    row_index = lax.axis_index("row")
    col_index = lax.axis_index("col")
    n_leaf = lax.axis_size("leaf")
    n_row = lax.axis_size("row")
    n_col = lax.axis_size("col")
    half = leaf_index % 2
    couple = leaf_index // 2
    nrhs = child_source.shape[2]
    half_dim, couple_dim = ("leaf", 0), ("leaf", 1)
    row_dims = bits_of("row")
    col_dims = bits_of("col")
    near_first = list(reversed(col_dims))

    child_rows, child_cols = child_inverse.shape[1:]
    middle_rows, middle_cols = middle_inverse.shape[1:]
    root_rows, root_cols = root_inverse.shape
    middle_first = (half * n_col + col_index) * middle_cols
    root_first = (leaf_index * n_col + col_index) * root_cols

    child_flags = lower_flags(
        child_diagmask[0], row_index * (child_rows // BLK), col_index * (child_cols // BLK)
    )
    middle_flags = lower_flags(
        middle_diagmask[0], row_index * (middle_rows // BLK), middle_first // BLK
    )
    root_flags = lower_flags(root_diagmask, row_index * (root_rows // BLK), root_first // BLK)
    child_upd_flags = child_updmask[0].reshape(-1)
    middle_upd_flags = middle_updmask[0].reshape(-1)

    child_lift_rows = child_update.shape[1]
    middle_lift_rows = middle_update.shape[1]
    pair_targets = lax.dynamic_slice_in_dim(child_rowmap, 2 * couple, 2, 0)
    pair_targets = pair_targets.reshape(2, n_col, n_row, child_lift_rows // n_row)
    pair_targets = lax.dynamic_index_in_dim(pair_targets, row_index, 2, False)
    pair_targets = relative(relative(pair_targets, 0, half), 1, col_index)
    pair_targets = pair_targets.transpose(1, 0, 2).reshape(-1) - middle_first
    root_targets = middle_rowmap.reshape(n_leaf, n_col, n_row, middle_lift_rows // n_row)
    root_targets = lax.dynamic_index_in_dim(root_targets, row_index, 2, False)
    root_targets = relative(relative(root_targets, 0, leaf_index), 1, col_index)
    root_targets = root_targets.transpose(1, 0, 2).reshape(-1) - root_first

    def chunked(panel, flags, x, plans, chunks, calls, update, update_flags):
        rows = panel.shape[0]
        count = 1 << len(plans[0])
        chunks = max(1, min(chunks, rows // (count * BLK)))
        unit = rows // chunks // count
        lift_order = block_order(row_dims, 0)
        plans = [plans[min(c, len(plans) - 1)] for c in range(chunks)]
        orders = [block_order(plans[c], c * count) for c in range(chunks)]
        partials = products_by_call(calls, chunks, panel, flags, x, orders, unit)
        values = [exchange_stages(*partials[c], plans[c]) for c in range(chunks)]
        places = [block_order(plans[c], 0) for c in range(chunks)]
        lift = None
        if chunks > 1:
            lift = update_product(
                update, update_flags, values[:-1], places[:-1], lift_order, 0
            )
        lift = update_product(
            update, update_flags, values[-1:], places[-1:], lift_order, chunks - 1, lift
        )

        def columns(first, width):
            if unit % BLK == 0:
                return turned_columns(values, places, first, width).T
            parts = [lax.dynamic_slice_in_dim(value, first, width, 1) for value in values]
            return jnp.concatenate(
                [in_order(part, plan) for part, plan in zip(parts, plans, strict=True)], 0
            )

        h = lift.shape[0] // 2
        return columns, reduce_scatter(lift[:h], lift[h:], row_dims)

    child_columns, child_lift = chunked(
        child_inverse[0], child_flags, child_source[0], [near_first], CHILD_CHUNKS, CHILD_CALLS,
        child_update[0], child_upd_flags,
    )
    pieces = []
    for piece in gather_line(child_lift, col_dims):
        pieces.append([piece, swapped(piece, half_dim)])
    added = placed_pieces(pieces, pair_targets, middle_cols, [n_col // 2])
    middle_rhs = middle_source[0] + row_sum(added, row_dims)

    middle_columns, middle_lift = chunked(
        middle_inverse[0], middle_flags, middle_rhs, [[half_dim] + near_first],
        MIDDLE_CHUNKS, MIDDLE_CALLS,
        middle_update[0], middle_upd_flags,
    )
    pieces = []
    for piece in gather_line(middle_lift, col_dims):
        h = piece.shape[0] // 2
        by_half = swapped(piece, half_dim)
        by_couple = swapped(piece, couple_dim)
        top = swapped(by_half[:h], couple_dim)
        bottom = swapped(by_couple[h:], half_dim)
        pieces.append([piece, by_half, by_couple, top, bottom])
    added = placed_pieces(pieces, root_targets, root_cols, [n_col // 2])
    root_rhs = root_source + row_sum(added, row_dims)

    chunks = max(2, min(ROOT_CHUNKS, root_rows // (4 * BLK)))
    unit = root_rows // chunks // 4
    share_width = nrhs // n_col
    pairs_count = chunks // 2
    col_order = block_order(near_first, 0, [1 << bit for _, bit in near_first])
    plans = [([half_dim, couple_dim], [1, 2]), ([couple_dim, half_dim], [2, 1])]

    def product_of(pair):
        size = 2 * unit if pair == 0 else unit
        orders = [block_order(plans[0][0], 0, plans[0][1])]
        if pair > 0:
            orders = [block_order(*plans[h][:1], (2 * pair + h) * 4, plans[h][1]) for h in range(2)]
        return panel_product(root_inverse, root_flags, root_rhs, orders, size)

    def col_sums(send, keep):
        for j, dim in enumerate(near_first):
            came = swapped(send, dim)
            if j < len(near_first) - 1:
                h = keep.shape[0] // 2
                send, keep = keep[:h] + came[:h], keep[h:] + came[h:]
        return keep, came

    order_of_pairs = range(pairs_count)
    products = {pair: product_of(pair) for pair in order_of_pairs}
    sums = []
    for pair in range(pairs_count):
        if pair == 0:
            send, keep = turned_sums(col_order, *products[0][0])
            keep, came = col_sums(send, keep)
            h = keep.shape[1] // 2
            send, keep = keep[:, :h] + came[:, :h], keep[:, h:] + came[:, h:]
            came = swapped(send, half_dim)
            h //= 2
            send, keep = keep[:, :h] + came[:, :h], keep[:, h:] + came[:, h:]
            came = swapped(send, couple_dim)
            sums.append(keep + came)
            continue
        seconds = []
        for h in range(2):
            (send, keep), (dims, _) = products[pair][h], plans[h]
            came = swapped(send, dims[0])
            send, keep = keep[:unit] + came[:unit], keep[unit:] + came[unit:]
            seconds += [keep, swapped(send, dims[1])]
        send, keep = turned_sums(col_order, *seconds)
        keep, came = col_sums(send, keep)
        sums.append(keep + came)
    gathers = ROOT_GATHERS if sum(ROOT_GATHERS) == pairs_count else (1,) * pairs_count
    root_out, first, late = None, 0, ([], [])
    for g, size in enumerate(gathers):
        pairs = range(first, first + size)
        first += size
        part = jnp.concatenate([sums[pair] for pair in pairs], 1)
        by_half = swapped(part, half_dim)
        by_couple = swapped(part, couple_dim)
        by_both = swapped(by_half, couple_dim) if g % 2 == 0 else swapped(by_couple, half_dim)
        pieces = [part, by_half, by_couple, by_both]
        if g == 0:
            root_out = finished_rows(pieces, [pairs], leaf_index, root_rows, None)
        else:
            late = (late[0] + pieces, late[1] + [pairs])
    if late[1]:
        root_out = finished_rows(*late, leaf_index, root_rows, root_out)

    child_out = child_columns(col_index * share_width, share_width)
    middle_width = nrhs // 2 // n_col
    middle_out = middle_columns(half * (nrhs // 2) + col_index * middle_width, middle_width)
    return (child_out[None], middle_out[None], root_out.T)


def solution(mesh):
    placed = (
        P("leaf", "col", None),
        P("leaf", "col", None),
        P(("leaf", "col"), None),
        P("leaf", "row", "col"),
        P("leaf", "col", "row"),
        P("leaf", "row", "col"),
        P("leaf", "col", "row"),
        P("row", ("leaf", "col")),
        P("leaf", "row", "col"),
        P("leaf", "col", "row"),
        P("leaf", "row", "col"),
        P("leaf", "col", "row"),
        P("row", ("leaf", "col")),
        P(),
        P(),
    )
    return jax.shard_map(
        local,
        mesh=mesh,
        in_specs=placed,
        out_specs=(P("leaf", "row", "col"), P("leaf", "row", "col"), P("row", "col")),
        check_vma=False,
    )
```
